32 devices in a mesh: pipe: 2 (over x), expert: 16 (over z, y, core).
Axes of the slice: x: 2, y: 2, z: 4, core: 2. Of those that a mesh axis runs over, the one named last changes fastest.
Arguments:
- front_tokens: bfloat16 [2, 192, 3584], P('pipe', 'expert'), may hold values from -6 to 6
- front_routes: int32 [2, 192, 2], P('pipe', 'expert'), may hold values from 0 to 1, all different within a row; in each aligned block of 12 rows (0 to 11, 12 to 23, ..., all dimensions but the last counted through in order) at most 12 rows name the same one
- front_mixing: int32 [2, 192, 2], P('pipe', 'expert'), may hold values from 1 to 15
- back_tokens: bfloat16 [2, 192, 3584], P('pipe', 'expert'), may hold values from -6 to 6
- back_routes: int32 [2, 192, 2], P('pipe', 'expert'), may hold values from 0 to 1, all different within a row; in each aligned block of 12 rows (0 to 11, 12 to 23, ..., all dimensions but the last counted through in order) at most 12 rows name the same one
- back_mixing: int32 [2, 192, 2], P('pipe', 'expert'), may hold values from 1 to 15
- back_upstream: bfloat16 [2, 192, 3584], P('pipe', 'expert'), may hold values from -6 to 6
- gate_weight: bfloat16 [2, 3584, 2048], P('pipe', None, 'expert'), may hold values from -0.09375 to 0.09375
- up_weight: bfloat16 [2, 3584, 2048], P('pipe', None, 'expert'), may hold values from -0.09375 to 0.09375
- down_weight: bfloat16 [2, 2048, 3584], P('pipe', 'expert'), may hold values from -0.1875 to 0.1875
Outputs:
- front_result: bfloat16 [2, 192, 3584], P('pipe', 'expert')
- token_grads: bfloat16 [2, 192, 3584], P('pipe', 'expert')
- gate_grads: bfloat16 [2, 1792, 2048], P('pipe', None, 'expert')
- up_grads: bfloat16 [2, 1792, 2048], P('pipe', None, 'expert')
- down_grads: bfloat16 [2, 2048, 1792], P('pipe', 'expert')
The draws below stay inside these ranges and needn't reach their ends.
Inputs may be any that keep to these rules, and one draw needn't show every extreme that they name: `front_routes`: each row names 2 different experts; within each device's block of 12 rows no expert is named more than 12 times, a bound that some block reaches. `back_routes`: each row names 2 different experts; within each device's block of 12 rows no expert is named more than 12 times, a bound that some block reaches.
All inputs are finite; a program needn't handle non-finite values.
Results may differ from the reference program's by a relative error of at most 0.0071.
Values may be sent and summed in bfloat16 or wider, within the bound.
A program may use at most 64 MiB of HBM per device.

```python
import math
import jax
import jax.numpy as jnp
import numpy as np
from jax import lax

D = 3584
FFW = 1024
SHARDS = 8
FFD = 128
TOP = 2
TOK_DEV = 12
EXPERTS = 2
CAP = 12
TOKENS = 192
N_PIPE = 2
N_EXPERT = 16


def touch_ends(entries, own_key, low, top_value):
    longest = entries.shape.index(max(entries.shape))
    spots = []
    for shift in (0, 1):
        where = [jax.random.randint(jax.random.fold_in(own_key, axis), (), 0, length) for axis, length in enumerate(entries.shape)]
        where[longest] = (where[longest] + shift) % entries.shape[longest]
        spots.append(tuple(where))
    return entries.at[spots[0]].set(low).at[spots[1]].set(top_value)


def level_of(rng, dims, split, low, high):
    gain = 1.0
    for axis_at, blocks in split:
        steps = jax.random.uniform(jax.random.fold_in(jax.random.fold_in(rng, 6), axis_at), (blocks,), jnp.float32, low / len(split), high / len(split))
        gain = gain * jnp.repeat(jnp.exp(steps), dims[axis_at] // blocks).reshape((-1,) + (1,) * (len(dims) - 1 - axis_at))
    return gain


def routed_block(key, own, number, rows, number_of, top, bound, lean):
    order = jax.random.permutation(key, number_of)
    packed, usual = load_shares(number_of, rows * top, bound, lean, True), load_shares(number_of, rows * top, bound, lean, False)
    places = jnp.arange(number_of)

    def named(lengths, offset_by):
        used = int((lengths > 0).sum())
        fixed = max(1, used // 4)
        shifted = fixed + (places - fixed + offset_by * (used - fixed)) % max(1, number_of - fixed)
        return jnp.zeros((number_of,), jnp.int32).at[order[jnp.where(places < fixed, places, shifted)]].set(jnp.asarray(lengths, jnp.int32))

    lengths = jnp.where(number % 4 == 0, named(packed, number // 4), named(usual, number - number // 4 - 1))
    mixed = jax.random.permutation(jax.random.fold_in(own, 3), number_of)
    donor, taker = mixed[0:number_of // 2 * 2:2], mixed[1:number_of // 2 * 2:2]
    margin = jnp.minimum(lengths[donor] - 1, bound - lengths[taker]) // 2
    margin = jnp.where((donor == order[0]) | (taker == order[0]) | (lengths[taker] == 0), 0, jnp.maximum(margin, 0))
    shifted = jax.random.randint(jax.random.fold_in(own, 4), (number_of // 2,), 0, 1 << 20) % (margin + 1)
    lengths = lengths.at[donor].add(-shifted).at[taker].add(shifted)
    items = jnp.searchsorted(jnp.cumsum(lengths), jnp.arange(rows * top), side="right").astype(jnp.int32)
    table = items.reshape(top, rows).T
    table = table[jax.random.permutation(jax.random.fold_in(own, 1), rows)]
    offset_by = jax.random.randint(jax.random.fold_in(own, 2), (rows, 1), 0, top)
    return jnp.take_along_axis(table, (jnp.arange(top)[None, :] + offset_by) % top, axis=1)


def load_shares(count, total, bound, skew, full):
    weights = [(1 << 20) // math.isqrt(grade ** skew) + 1 for grade in range(1, count + 1)]
    largest = bound if full else min(bound, max(-(-total // count), total * weights[0] // sum(weights)))
    least = 1 if total - largest >= count - 1 else 0
    given, surplus = [largest] + [least] * (count - 1), total - largest - least * (count - 1)
    while surplus > 0:
        candidates = [i for i in range(1, count) if given[i] < largest] or [i for i in range(1, count) if given[i] < bound]
        whole, left = sum([weights[i] for i in candidates]), surplus
        for i in candidates:
            extra = min(bound - given[i], max(1, left * weights[i] // whole), surplus)
            given[i] = given[i] + extra
            surplus = surplus - extra
    return np.array(given)


def normal_values(stream_key, dims, scale, bound, cuts=(), held_as=jnp.bfloat16):
    factor_of = level_of(stream_key, dims, cuts, -0.22, 0.18) if cuts else 1.0
    result = jax.random.normal(stream_key, dims, jnp.float32) * scale * factor_of
    return jnp.minimum(jnp.maximum(result, -bound), bound).astype(held_as)


def setup_inputs(seed: int = 0) -> dict:
    arg_keys = jax.random.split(jax.random.key(seed), 11)
    front_tokens = normal_values(arg_keys[0], (N_PIPE, TOKENS, D), 1.0, 6.0, ((0, 2), (1, 16)))
    front_routes_keys = jax.random.split(jax.random.fold_in(arg_keys[1], 1), N_PIPE * TOKENS // TOK_DEV)
    front_routes_turns = jax.random.permutation(jax.random.fold_in(arg_keys[1], 3), N_PIPE * TOKENS // TOK_DEV)
    front_routes = jax.vmap(lambda own, number: routed_block(jax.random.fold_in(arg_keys[1], 2), own, number, TOK_DEV, EXPERTS, TOP, CAP, 0))(front_routes_keys, front_routes_turns).reshape((N_PIPE, TOKENS, TOP))
    front_mixing = touch_ends(jax.random.randint(arg_keys[2], (N_PIPE, TOKENS, TOP), 1, 16), jax.random.fold_in(arg_keys[2], 1), 1, 15).astype(jnp.int32)
    back_tokens = normal_values(arg_keys[3], (N_PIPE, TOKENS, D), 1.0, 6.0, ((0, 2), (1, 16)))
    back_routes_keys = jax.random.split(jax.random.fold_in(arg_keys[4], 1), N_PIPE * TOKENS // TOK_DEV)
    back_routes_turns = jax.random.permutation(jax.random.fold_in(arg_keys[4], 3), N_PIPE * TOKENS // TOK_DEV)
    back_routes = jax.vmap(lambda own, number: routed_block(jax.random.fold_in(arg_keys[4], 2), own, number, TOK_DEV, EXPERTS, TOP, CAP, 0))(back_routes_keys, back_routes_turns).reshape((N_PIPE, TOKENS, TOP))
    back_mixing = touch_ends(jax.random.randint(arg_keys[5], (N_PIPE, TOKENS, TOP), 1, 16), jax.random.fold_in(arg_keys[5], 1), 1, 15).astype(jnp.int32)
    back_upstream = normal_values(arg_keys[6], (N_PIPE, TOKENS, D), 1.0, 6.0, ((0, 2), (1, 16)))
    gate_weight = normal_values(arg_keys[7], (N_PIPE, D, EXPERTS * FFW), D ** -0.5, 0.09375, ((0, 2), (2, 16)))
    up_weight = normal_values(arg_keys[8], (N_PIPE, D, EXPERTS * FFW), D ** -0.5, 0.09375, ((0, 2), (2, 16)))
    down_weight = normal_values(arg_keys[9], (N_PIPE, EXPERTS * FFW, D), FFW ** -0.5, 0.1875, ((0, 2), (1, 16)))
    return {"front_tokens": front_tokens, "front_routes": front_routes, "front_mixing": front_mixing, "back_tokens": back_tokens, "back_routes": back_routes, "back_mixing": back_mixing, "back_upstream": back_upstream, "gate_weight": gate_weight, "up_weight": up_weight, "down_weight": down_weight}


weight_unit = 0.0625


def slot_table(routes):
    per_block = routes.reshape(N_EXPERT, TOK_DEV * TOP)
    matches = (per_block[:, :, None] == jnp.arange(EXPERTS, dtype=jnp.int32)[None, None, :]).astype(jnp.int32)
    earlier = jnp.cumsum(matches, axis=1) - matches
    position = jnp.sum(earlier * matches, axis=2)
    blocks = jnp.arange(N_EXPERT, dtype=jnp.int32)[:, None]
    return (blocks * CAP + position).reshape(TOKENS, TOP).astype(jnp.int32)


def scatter_rows(values, routes, slot_index):
    buffer = jnp.zeros((EXPERTS, N_EXPERT * CAP, D), values.dtype)
    return buffer.at[routes, slot_index].set(values)


def barrier_float(values):
    return lax.optimization_barrier(values).astype(jnp.float32)


def shard_total(shard_parts):
    return jnp.sum(barrier_float(shard_parts.astype(jnp.bfloat16)), axis=0).astype(jnp.bfloat16)


def forward_expert(operands):
    tok_rows, gate_cols, up_cols, down_rows = operands
    gate_val = jnp.dot(tok_rows, gate_cols, preferred_element_type=jnp.float32)
    up_val = jnp.dot(tok_rows, up_cols, preferred_element_type=jnp.float32)
    hidden = (jax.nn.silu(gate_val) * up_val).astype(jnp.bfloat16)
    split_hidden = barrier_float(hidden).reshape(-1, SHARDS, FFD)
    split_down = down_rows.astype(jnp.float32).reshape(SHARDS, FFD, D)
    shard_parts = jnp.einsum("rsf,sfd->srd", split_hidden, split_down)
    return shard_total(shard_parts)


def backward_expert(operands):
    tok_rows, scaled_rows, gate_cols, up_cols, down_rows = operands
    gate_val = jnp.dot(tok_rows, gate_cols, preferred_element_type=jnp.float32)
    up_val = jnp.dot(tok_rows, up_cols, preferred_element_type=jnp.float32)
    gate_act = jax.nn.silu(gate_val)
    gate_sig = jax.nn.sigmoid(gate_val)
    hidden = (gate_act * up_val).astype(jnp.bfloat16)
    down_grad = jnp.dot(hidden.T, scaled_rows, preferred_element_type=jnp.float32).astype(jnp.bfloat16)
    hidden_grad = jnp.dot(scaled_rows, down_rows.T, preferred_element_type=jnp.float32)
    act_slope = gate_sig * (1.0 + gate_val * (1.0 - gate_sig))
    gate_delta = (hidden_grad * up_val * act_slope).astype(jnp.bfloat16)
    up_delta = (hidden_grad * gate_act).astype(jnp.bfloat16)
    gate_grad = jnp.dot(tok_rows.T, gate_delta, preferred_element_type=jnp.float32).astype(jnp.bfloat16)
    up_grad = jnp.dot(tok_rows.T, up_delta, preferred_element_type=jnp.float32).astype(jnp.bfloat16)
    split_gate = barrier_float(gate_delta).reshape(-1, SHARDS, FFD)
    split_up = barrier_float(up_delta).reshape(-1, SHARDS, FFD)
    gate_shards = gate_cols.astype(jnp.float32).reshape(D, SHARDS, FFD)
    up_shards = up_cols.astype(jnp.float32).reshape(D, SHARDS, FFD)
    shard_parts = jnp.einsum("rsf,dsf->srd", split_gate, gate_shards) + jnp.einsum("rsf,dsf->srd", split_up, up_shards)
    return shard_total(shard_parts), gate_grad, up_grad, down_grad


def reference(front_tokens, front_routes, front_mixing, back_tokens, back_routes, back_mixing, back_upstream, gate_weight, up_weight, down_weight):
    front_list = []
    token_list = []
    grads_list = []
    for section_index in range(N_PIPE):
        gate_all = gate_weight[section_index].reshape(D, EXPERTS, FFW).transpose(1, 0, 2)
        up_all = up_weight[section_index].reshape(D, EXPERTS, FFW).transpose(1, 0, 2)
        down_all = down_weight[section_index].reshape(EXPERTS, FFW, D)

        routes = front_routes[section_index]
        slot_index = slot_table(routes)
        mixing = front_mixing[section_index].astype(jnp.float32) * weight_unit
        copied_rows = jnp.broadcast_to(front_tokens[section_index][:, None, :], (TOKENS, TOP, D))
        front_rows = scatter_rows(copied_rows, routes, slot_index)
        front_slots = lax.map(forward_expert, (front_rows, gate_all, up_all, down_all))
        picked = front_slots[routes, slot_index].astype(jnp.float32)
        front_list.append(jnp.sum(mixing[:, :, None] * picked, axis=1).astype(jnp.bfloat16))

        routes = back_routes[section_index]
        slot_index = slot_table(routes)
        mixing = back_mixing[section_index].astype(jnp.float32) * weight_unit
        copied_rows = jnp.broadcast_to(back_tokens[section_index][:, None, :], (TOKENS, TOP, D))
        back_rows = scatter_rows(copied_rows, routes, slot_index)
        scaled = (mixing[:, :, None] * back_upstream[section_index].astype(jnp.float32)[:, None, :]).astype(jnp.bfloat16)
        scaled_rows = scatter_rows(scaled, routes, slot_index)
        grad_slots, gate_section, up_section, down_section = lax.map(backward_expert, (back_rows, scaled_rows, gate_all, up_all, down_all))
        picked = grad_slots[routes, slot_index].astype(jnp.float32)
        token_list.append(jnp.sum(picked, axis=1).astype(jnp.bfloat16))
        grads_list.append((gate_section.transpose(1, 0, 2).reshape(D, EXPERTS * FFW), up_section.transpose(1, 0, 2).reshape(D, EXPERTS * FFW), down_section.reshape(EXPERTS * FFW, D)))

    half_rows = D // 2
    gate_out = []
    up_out = []
    down_out = []
    for section_index in range(N_PIPE):
        mirror = N_PIPE - 1 - section_index
        start_row = half_rows if 2 * section_index >= N_PIPE else 0
        gate_sum = (barrier_float(grads_list[section_index][0]) + barrier_float(grads_list[mirror][0])).astype(jnp.bfloat16)
        up_sum = (barrier_float(grads_list[section_index][1]) + barrier_float(grads_list[mirror][1])).astype(jnp.bfloat16)
        down_sum = (barrier_float(grads_list[section_index][2]) + barrier_float(grads_list[mirror][2])).astype(jnp.bfloat16)
        gate_out.append(gate_sum[start_row:start_row + half_rows])
        up_out.append(up_sum[start_row:start_row + half_rows])
        down_out.append(down_sum[:, start_row:start_row + half_rows])
    return (jnp.stack(front_list), jnp.stack(token_list), jnp.stack(gate_out), jnp.stack(up_out), jnp.stack(down_out))
```

```python
import jax
import jax.numpy as jnp
from jax import lax
from jax.sharding import PartitionSpec as P

SHARDS = 8
LANES = 128

weight_unit = 0.0625


def token_weights(routes, mixing):
    hits = routes[:, :, None] == jnp.arange(LANES, dtype=jnp.int32)[None, None, :]
    weights = mixing.astype(jnp.float32) * weight_unit
    return jnp.sum(jnp.where(hits, weights[:, :, None], 0.0), axis=1).astype(jnp.bfloat16)


def rows_dot(rows, matrix, dim):
    return lax.dot_general(
        rows, matrix, (((2,), (dim,)), ((), ())), preferred_element_type=jnp.float32
    )


def grad_dot(rows, deltas):
    return lax.dot_general(
        rows, deltas, (((0, 1), (0, 1)), ((), ())), preferred_element_type=jnp.float32
    ).astype(jnp.bfloat16)


def local(
    front_tokens,
    front_routes,
    front_mixing,
    back_tokens,
    back_routes,
    back_mixing,
    back_upstream,
    gate_weight,
    up_weight,
    down_weight,
):
    tokens = front_tokens.shape[1]
    features = front_tokens.shape[2]
    gate_cols = gate_weight[0]
    up_cols = up_weight[0]
    down_rows = down_weight[0]
    expert = lax.axis_index("expert") // SHARDS
    picked = (jnp.arange(LANES, dtype=jnp.int32) == expert).astype(jnp.float32)

    front_table = token_weights(front_routes[0], front_mixing[0])
    back_table = token_weights(back_routes[0], back_mixing[0])
    back_load = jnp.concatenate(
        [
            jnp.concatenate([back_tokens[0], jnp.zeros_like(back_table)], axis=1),
            jnp.concatenate([back_upstream[0], back_table], axis=1),
        ],
        axis=0,
    )
    front_load = jnp.concatenate([front_tokens[0], front_table], axis=1)
    back_all = lax.all_gather(back_load, "expert", axis=0)
    front_all = lax.all_gather(front_load, "expert", axis=0)

    def own_weight(table):
        return jnp.sum(table.astype(jnp.float32) * picked, axis=2, keepdims=True)

    back_rows = back_all[:, :tokens, :features]
    upstream = back_all[:, tokens:, :features]
    back_scale = own_weight(back_all[:, tokens:, features:])
    scaled_rows = (upstream.astype(jnp.float32) * back_scale).astype(jnp.bfloat16)
    back_gate = rows_dot(back_rows, gate_cols, 0)
    back_up = rows_dot(back_rows, up_cols, 0)
    hidden_grad = rows_dot(scaled_rows, down_rows, 1)
    gate_sig = jax.nn.sigmoid(back_gate)
    gate_act = back_gate * gate_sig
    back_hidden = (gate_act * back_up).astype(jnp.bfloat16)
    act_slope = gate_sig * (1.0 + back_gate * (1.0 - gate_sig))
    gate_delta = (hidden_grad * back_up * act_slope).astype(jnp.bfloat16)
    up_delta = (hidden_grad * gate_act).astype(jnp.bfloat16)
    sections = jnp.stack(
        [
            grad_dot(back_rows, gate_delta),
            grad_dot(back_rows, up_delta),
            grad_dot(scaled_rows, back_hidden),
        ]
    )
    pipe_count = lax.axis_size("pipe")
    half = features // 2
    upper = lax.axis_index("pipe") * 2 >= pipe_count
    own_start = jnp.where(upper, half, 0)
    own_half = lax.dynamic_slice_in_dim(sections, own_start, half, axis=1)
    leaving = lax.dynamic_slice_in_dim(sections, half - own_start, half, axis=1)
    arrived = lax.ppermute(leaving, "pipe", [(p, pipe_count - 1 - p) for p in range(pipe_count)])

    back_parts = (rows_dot(gate_delta, gate_cols, 1) + rows_dot(up_delta, up_cols, 1)).astype(
        jnp.bfloat16
    )
    front_rows = front_all[:, :, :features]
    front_scale = own_weight(front_all[:, :, features:])
    front_gate = rows_dot(front_rows, gate_cols, 0)
    front_up = rows_dot(front_rows, up_cols, 0)
    front_hidden = (jax.nn.silu(front_gate) * front_up).astype(jnp.bfloat16)
    front_parts = (rows_dot(front_hidden, down_rows, 0) * front_scale).astype(jnp.bfloat16)
    totals = lax.psum_scatter(
        jnp.concatenate([front_parts, back_parts], axis=1), "expert", scatter_dimension=0
    )
    summed = (own_half.astype(jnp.float32) + arrived.astype(jnp.float32)).astype(jnp.bfloat16)
    return (
        totals[:tokens][None],
        totals[tokens:][None],
        summed[0][None],
        summed[1][None],
        summed[2].T[None],
    )


def solution(mesh):
    rows = P("pipe", "expert", None)
    columns = P("pipe", None, "expert")
    return jax.shard_map(
        local,
        mesh=mesh,
        in_specs=(rows,) * 7 + (columns, columns, rows),
        out_specs=(rows, rows, columns, columns, rows),
        check_vma=False,
    )
```
